32 devices in a mesh: dp: 4 (over x, core), ctx: 4 (over z), tensor: 2 (over y).
Axes of the slice: x: 2, y: 2, z: 4, core: 2. Of those that a mesh axis runs over, the one named last changes fastest.
Arguments:
- tokens: bfloat16 [4, 1024, 1024], P('dp', 'ctx'), may hold values from -6 to 6
- seq_lengths: int32 [4], P('dp'), may hold values from 256 to 1024, as said below
- qkv_weight: bfloat16 [1024, 3, 1024], P(('dp', 'ctx'), None, 'tensor'), may hold values from -4 to 4
- out_weight: bfloat16 [1024, 1024], P(('dp', 'ctx'), 'tensor'), may hold values from -1.5 to 1.5
- up_weight: bfloat16 [1024, 4096], P(('dp', 'ctx'), 'tensor'), may hold values from -0.1875 to 0.1875
- down_weight: bfloat16 [1024, 4096], P(('dp', 'ctx'), 'tensor'), may hold values from -0.09375 to 0.09375
- head_bias: bfloat16 [16, 128], P('tensor', ('dp', 'ctx')), may hold values from -3 to 3
- hidden_bias: bfloat16 [32, 128], P('tensor', ('dp', 'ctx')), may hold values from -3 to 3
- norm_gains: bfloat16 [2, 1024], P(None, ('dp', 'ctx')), may hold values from 0.25 to 1.75
- out_biases: bfloat16 [4, 1024], P(None, ('dp', 'ctx')), may hold values from -3 to 3
- cotangent: bfloat16 [4, 1024, 1024], P('dp', 'ctx'), may hold values from -6 to 6
Outputs:
- output: bfloat16 [4, 1024, 1024], P('dp', 'ctx')
- input_grad: float32 [4, 1024, 1024], P('dp', 'ctx')
- qkv_grad: float32 [1024, 3, 1024], P(('dp', 'ctx'), None, 'tensor')
- out_weight_grad: float32 [1024, 1024], P(('dp', 'ctx'), 'tensor')
- up_grad: float32 [1024, 4096], P(('dp', 'ctx'), 'tensor')
- down_grad: float32 [1024, 4096], P(('dp', 'ctx'), 'tensor')
- head_bias_grad: float32 [16, 128], P('tensor', ('dp', 'ctx'))
- hidden_bias_grad: float32 [32, 128], P('tensor', ('dp', 'ctx'))
- gains_grad: float32 [2, 1024], P(None, ('dp', 'ctx'))
- biases_grad: float32 [4, 1024], P(None, ('dp', 'ctx'))
The draws below stay inside these ranges and needn't reach their ends.
Inputs may be any that keep to these rules, and one draw needn't show every extreme that they name: `seq_lengths`: valid tokens of each sequence; in every draw some sequence has exactly 1024.
All inputs are finite; a program needn't handle non-finite values.
Results may differ from the reference program's by a relative error of at most 0.011.
The reference program's roundings to bfloat16 on the way count: a program that leaves them out, or rounds other values in their place, can miss the bound.
Values may be sent and summed in bfloat16 or wider, within the bound.
A program may use at most 128 MiB of HBM per device.

```python
import math
import jax
import jax.numpy as jnp
from jax import lax

D = 1024
H = 16
HD = 64
FF = 4096
L = 1024
SEQS = 4


def draw_tokens(key, part):
    values = jax.random.normal(key, (SEQS, L, D), jnp.float32)
    return jnp.clip(values, -6.0, 6.0).astype(jnp.bfloat16)


def draw_qkv_weight(key, part):
    base = jax.random.normal(key, (D, 3, D), jnp.float32) * D ** (-0.5)
    return jnp.clip(base, -4.0, 4.0).astype(jnp.bfloat16)


def draw_seq_lengths(key, part):
    lengths = jax.random.randint(key, (SEQS,), L // 4, L + 1, dtype=jnp.int32)
    chosen = jax.random.randint(jax.random.fold_in(key, 5), (), 0, SEQS, dtype=jnp.int32)
    return jnp.where(jnp.arange(SEQS) == chosen, L, lengths).astype(jnp.int32)


def block_levels(key, extent, pieces, smallest, top_value):
    loudness, own = 1.0, jax.random.fold_in(key, 6)
    for axis_at, parts in pieces:
        steps = jnp.exp(jax.random.uniform(jax.random.fold_in(own, axis_at), (parts,), jnp.float32, smallest / len(pieces), top_value / len(pieces)))
        loudness = loudness * jnp.repeat(steps, extent[axis_at] // parts).reshape([-1 if axis == axis_at else 1 for axis in range(len(extent))])
    return loudness


def gaussian(rng, extent, scale, limit, shards=(), kind=jnp.bfloat16):
    entries = jax.random.normal(rng, extent, jnp.float32) * scale
    if len(shards) > 0:
        entries = block_levels(rng, extent, shards, -0.22, 0.18) * entries
    return jnp.clip(entries, min=-limit, max=limit).astype(kind)


def setup_inputs(seed: int = 0) -> dict:
    splits = jax.random.split(jax.random.key(seed), 12)
    return {
        "tokens": draw_tokens(jax.random.fold_in(splits[11], 71), 0),
        "seq_lengths": draw_seq_lengths(jax.random.fold_in(splits[11], 71), 0),
        "qkv_weight": draw_qkv_weight(jax.random.fold_in(splits[11], 71), 0),
        "out_weight": gaussian(splits[3], (D, D), (D // 64) ** -0.5, 1.5, ((0, 16), (1, 2))),
        "up_weight": gaussian(splits[4], (D, FF), D ** -0.5, 0.1875, ((0, 16), (1, 2))),
        "down_weight": gaussian(splits[5], (D, FF), FF ** -0.5, 0.09375, ((0, 16), (1, 2))),
        "head_bias": gaussian(splits[6], (H, 2 * HD), 0.5, 3.0, ((0, 2), (1, 16))),
        "hidden_bias": gaussian(splits[7], (FF // (2 * HD), 2 * HD), 0.5, 3.0, ((0, 2), (1, 16))),
        "norm_gains": jnp.clip(1.0 + 0.15 * jax.random.normal(splits[8], (2, D), jnp.float32), 0.25, 1.75).astype(jnp.bfloat16),
        "out_biases": gaussian(splits[9], (4, D), 0.5, 3.0, ((1, 16),)),
        "cotangent": gaussian(splits[10], (SEQS, L, D), 1.0, 6.0, ((0, 4), (1, 4))),
    }


EPSILON = 1e-05
SCALE = 0.125
NEG_BIG = -1000000000.0
INV_ROOT_TWO = 1.0 / math.sqrt(2.0)
INV_ROOT_TWO_PI = 1.0 / math.sqrt(2.0 * math.pi)

def low_f32(values):
    return lax.optimization_barrier(values.astype(jnp.bfloat16)).astype(jnp.float32)

def layer_norm(hidden_in, gain, shift):
    centred = hidden_in - lax.optimization_barrier(jnp.mean(hidden_in, axis=-1, keepdims=True))
    variance = lax.optimization_barrier(jnp.mean(centred * centred, axis=-1, keepdims=True))
    inv_std = lax.rsqrt(variance + EPSILON)
    normed = centred * inv_std
    return (normed * gain + shift, normed, inv_std)

def norm_back(grad_out, normed, inv_std, gain):
    grad_normed = grad_out * gain
    first_mean = lax.optimization_barrier(jnp.mean(grad_normed, axis=-1, keepdims=True))
    second_mean = lax.optimization_barrier(jnp.mean(grad_normed * normed, axis=-1, keepdims=True))
    grad_in = inv_std * (grad_normed - first_mean - normed * second_mean)
    return (grad_in, lax.optimization_barrier(jnp.sum(grad_out * normed, axis=0)), lax.optimization_barrier(jnp.sum(grad_out, axis=0)))

def gelu_parts(pre_act):
    cdf_val = 0.5 * (1.0 + jax.scipy.special.erf(pre_act * INV_ROOT_TWO))
    return (pre_act * cdf_val, cdf_val + pre_act * jnp.exp(-0.5 * pre_act * pre_act) * INV_ROOT_TWO_PI)

def ref_scores(queries, key_rows, valid):
    scores = jnp.einsum('qhd,khd->hqk', queries.astype(jnp.float32), key_rows.astype(jnp.float32)) * SCALE
    return jnp.where(valid[None, None, :], scores, NEG_BIG)

def ref_attend(queries, key_rows, value_rows, valid):
    scores = ref_scores(queries, key_rows, valid)
    peak = lax.optimization_barrier(jnp.max(scores, axis=-1, keepdims=True))
    log_total = peak + jnp.log(lax.optimization_barrier(jnp.sum(jnp.exp(scores - peak), axis=-1, keepdims=True)))
    probs = low_f32(jnp.exp(scores - log_total))
    mixed = jnp.einsum('hqk,khd->qhd', probs, value_rows.astype(jnp.float32)).astype(jnp.bfloat16)
    return (mixed, log_total)

def ref_attend_back(queries, key_rows, value_rows, valid, mixed, log_total, grad_mixed):
    scores = ref_scores(queries, key_rows, valid)
    probs = jnp.exp(scores - log_total)
    grad_wide = grad_mixed.astype(jnp.float32)
    grad_values = jnp.einsum('hqk,qhd->khd', low_f32(probs), grad_wide)
    grad_probs = jnp.einsum('qhd,khd->hqk', grad_wide, value_rows.astype(jnp.float32))
    inner = jnp.einsum('qhd,qhd->hq', grad_wide, mixed.astype(jnp.float32))
    grad_scores = low_f32(probs * (grad_probs - inner[:, :, None]))
    grad_queries = jnp.einsum('hqk,khd->qhd', grad_scores, key_rows.astype(jnp.float32)) * SCALE
    grad_keys = jnp.einsum('hqk,qhd->khd', grad_scores, queries.astype(jnp.float32)) * SCALE
    return (grad_queries, grad_keys, grad_values)

def reference(tokens, seq_lengths, qkv_weight, out_weight, up_weight, down_weight, head_bias, hidden_bias, norm_gains, out_biases, cotangent):
    qkv_flat = qkv_weight.reshape(D, 3 * D)
    bias_query = head_bias[:, :HD].reshape(D).astype(jnp.float32)
    bias_value = head_bias[:, HD:].reshape(D).astype(jnp.float32)
    bias_hidden = hidden_bias.reshape(FF).astype(jnp.float32)
    gains_wide = norm_gains.astype(jnp.float32)
    biases_wide = out_biases.astype(jnp.float32)
    positions = jnp.arange(L)

    def one_sequence(carry, inputs):
        seq_tokens, seq_cot, length = inputs
        valid = positions < length
        projected = jnp.dot(seq_tokens, qkv_flat, preferred_element_type=jnp.float32).reshape(L, 3, D)
        queries = (projected[:, 0] + bias_query).astype(jnp.bfloat16).reshape(L, H, HD)
        key_rows = projected[:, 1].astype(jnp.bfloat16).reshape(L, H, HD)
        value_rows = (projected[:, 2] + bias_value).astype(jnp.bfloat16).reshape(L, H, HD)
        mixed, log_total = ref_attend(queries, key_rows, value_rows, valid)
        attn_flat = mixed.reshape(L, D)
        attn_proj = jnp.dot(attn_flat, out_weight.T, preferred_element_type=jnp.float32)
        first_sum = seq_tokens.astype(jnp.float32) + attn_proj + biases_wide[0]
        normed_one, z_one, rstd_one = layer_norm(first_sum, gains_wide[0], biases_wide[1])
        normed_low = normed_one.astype(jnp.bfloat16)
        pre_act = jnp.dot(normed_low, up_weight, preferred_element_type=jnp.float32) + bias_hidden
        activated, slope = gelu_parts(pre_act)
        hidden_low = activated.astype(jnp.bfloat16)
        mlp_out = jnp.dot(hidden_low, down_weight.T, preferred_element_type=jnp.float32)
        second_sum = normed_one + mlp_out + biases_wide[2]
        result, z_two, rstd_two = layer_norm(second_sum, gains_wide[1], biases_wide[3])
        output_rows = result.astype(jnp.bfloat16)
        grad_out = seq_cot.astype(jnp.float32)
        grad_two, gain_two_grad, shift_two_grad = norm_back(grad_out, z_two, rstd_two, gains_wide[1])
        grad_two_low = grad_two.astype(jnp.bfloat16)
        down_part = jnp.dot(grad_two_low.T, hidden_low, preferred_element_type=jnp.float32)
        grad_hidden = jnp.dot(grad_two_low, down_weight, preferred_element_type=jnp.float32)
        grad_pre = grad_hidden * slope
        grad_pre_low = grad_pre.astype(jnp.bfloat16)
        up_part = jnp.dot(normed_low.T, grad_pre_low, preferred_element_type=jnp.float32)
        grad_normed = jnp.dot(grad_pre_low, up_weight.T, preferred_element_type=jnp.float32) + grad_two
        grad_one, gain_one_grad, shift_one_grad = norm_back(grad_normed, z_one, rstd_one, gains_wide[0])
        grad_one_low = grad_one.astype(jnp.bfloat16)
        out_part = jnp.dot(grad_one_low.T, attn_flat, preferred_element_type=jnp.float32)
        grad_attn = jnp.dot(grad_one_low, out_weight, preferred_element_type=jnp.float32).astype(jnp.bfloat16)
        grad_queries, grad_keys, grad_values = ref_attend_back(queries, key_rows, value_rows, valid, mixed, log_total, grad_attn.reshape(L, H, HD))
        grad_queries = grad_queries.reshape(L, D)
        grad_values = grad_values.reshape(L, D)
        grad_proj = jnp.stack([grad_queries, grad_keys.reshape(L, D), grad_values], axis=1).astype(jnp.bfloat16).reshape(L, 3 * D)
        qkv_part = jnp.dot(seq_tokens.T, grad_proj, preferred_element_type=jnp.float32)
        input_rows = jnp.dot(grad_proj, qkv_flat.T, preferred_element_type=jnp.float32) + grad_one
        terms = (qkv_part, out_part, up_part, down_part, lax.optimization_barrier(jnp.sum(grad_queries, axis=0)), lax.optimization_barrier(jnp.sum(grad_values, axis=0)), lax.optimization_barrier(jnp.sum(grad_pre, axis=0)), jnp.stack([gain_one_grad, gain_two_grad]), jnp.stack([lax.optimization_barrier(jnp.sum(grad_one, axis=0)), shift_one_grad, lax.optimization_barrier(jnp.sum(grad_two, axis=0)), shift_two_grad]))
        new_carry = tuple((total + term for total, term in zip(carry, terms)))
        return (new_carry, (output_rows, input_rows))
    start = (jnp.zeros((D, 3 * D), jnp.float32), jnp.zeros((D, D), jnp.float32), jnp.zeros((D, FF), jnp.float32), jnp.zeros((D, FF), jnp.float32), jnp.zeros((D,), jnp.float32), jnp.zeros((D,), jnp.float32), jnp.zeros((FF,), jnp.float32), jnp.zeros((2, D), jnp.float32), jnp.zeros((4, D), jnp.float32))
    totals, (output, input_grad) = lax.scan(one_sequence, start, (tokens, cotangent, seq_lengths))
    qkv_grad = totals[0].reshape(D, 3, D)
    head_bias_grad = jnp.concatenate([totals[4].reshape(H, HD), totals[5].reshape(H, HD)], axis=1)
    hidden_bias_grad = totals[6].reshape(FF // (2 * HD), 2 * HD)
    return (output, input_grad, qkv_grad, totals[1], totals[2], totals[3], head_bias_grad, hidden_bias_grad, totals[7], totals[8])
```

```python
import functools
import math

import jax
import jax.numpy as jnp
from jax import lax
from jax.experimental import pallas as pl
from jax.experimental.pallas import tpu as pltpu
from jax.sharding import PartitionSpec as P

EPSILON = 1e-05
SCALE = 0.125
NEG_BIG = -1000000000.0
INV_ROOT_TWO = 1.0 / math.sqrt(2.0)
INV_ROOT_TWO_PI = 1.0 / math.sqrt(2.0 * math.pi)


def contract_last(left, right):
    return lax.dot_general(
        left, right, (((1,), (1,)), ((), ())), preferred_element_type=jnp.float32
    )


def contract_first(left, right):
    return lax.dot_general(
        left, right, (((0,), (0,)), ((), ())), preferred_element_type=jnp.float32
    )


def layer_norm(hidden_in, gain, shift):
    centred = hidden_in - jnp.mean(hidden_in, axis=-1, keepdims=True)
    variance = jnp.mean(centred * centred, axis=-1, keepdims=True)
    inv_std = lax.rsqrt(variance + EPSILON)
    normed = centred * inv_std
    return (normed * gain + shift, normed, inv_std)


def norm_back(grad_out, normed, inv_std, gain):
    grad_normed = grad_out * gain
    first_mean = jnp.mean(grad_normed, axis=-1, keepdims=True)
    second_mean = jnp.mean(grad_normed * normed, axis=-1, keepdims=True)
    grad_in = inv_std * (grad_normed - first_mean - normed * second_mean)
    return (grad_in, jnp.sum(grad_out * normed, axis=0), jnp.sum(grad_out, axis=0))


def gelu_parts(pre_act):
    cdf_val = 0.5 * (1.0 + jax.scipy.special.erf(pre_act * INV_ROOT_TWO))
    return (
        pre_act * cdf_val,
        cdf_val + pre_act * jnp.exp(-0.5 * pre_act * pre_act) * INV_ROOT_TWO_PI,
    )


def block_scores(queries, key_rows, valid):
    scores = (
        jnp.einsum("qhd,khd->hqk", queries, key_rows, preferred_element_type=jnp.float32) * SCALE
    )
    return jnp.where(valid[None, None, :], scores, NEG_BIG)


def attend_forward(inputs):
    queries, key_rows, value_rows, valid = inputs
    scores = block_scores(queries, key_rows, valid)
    peak = jnp.max(scores, axis=-1, keepdims=True)
    log_total = peak + jnp.log(jnp.sum(jnp.exp(scores - peak), axis=-1, keepdims=True))
    probs = jnp.exp(scores - log_total).astype(jnp.bfloat16)
    mixed = jnp.einsum(
        "hqk,khd->qhd", probs, value_rows, preferred_element_type=jnp.float32
    ).astype(jnp.bfloat16)
    return (mixed, log_total)


def attend_backward(inputs):
    queries, key_rows, value_rows, valid, mixed, log_total, grad_mixed = inputs
    scores = block_scores(queries, key_rows, valid)
    probs = jnp.exp(scores - log_total)
    grad_values = jnp.einsum(
        "hqk,qhd->khd", probs.astype(jnp.bfloat16), grad_mixed, preferred_element_type=jnp.float32
    )
    grad_probs = jnp.einsum(
        "qhd,khd->hqk", grad_mixed, value_rows, preferred_element_type=jnp.float32
    )
    inner = jnp.einsum("qhd,qhd->hq", grad_mixed.astype(jnp.float32), mixed.astype(jnp.float32))
    grad_scores = (probs * (grad_probs - inner[:, :, None])).astype(jnp.bfloat16)
    grad_queries = (
        jnp.einsum("hqk,khd->qhd", grad_scores, key_rows, preferred_element_type=jnp.float32)
        * SCALE
    )
    grad_keys = (
        jnp.einsum("hqk,qhd->khd", grad_scores, queries, preferred_element_type=jnp.float32) * SCALE
    )
    return (grad_queries, grad_keys, grad_values)


def comm_kernel(sizes, kinds, copies, *refs):
    n_outer, n_core, n_ctx, n_tensor = sizes
    count = len(kinds)
    ins, outs = refs[:count], refs[count : 2 * count]
    send_sem, recv_sem, own_sem = refs[2 * count :]
    dp, ctx, tensor = (lax.axis_index(name) for name in ("dp", "ctx", "tensor"))
    outer, core = dp // n_core, dp % n_core

    def coords(offset, sign=1):
        def move(at, step, size):
            return at if step == 0 else (at + (step if sign > 0 else size - step)) % size

        outer_at = move(outer, offset[0], n_outer)
        core_at = move(core, offset[1], n_core)
        return outer_at * n_core + core_at, move(ctx, offset[2], n_ctx), move(tensor, offset[3], n_tensor)

    def device(offset):
        dp_at, ctx_at, tensor_at = coords(offset)
        return {"dp": dp_at, "ctx": ctx_at, "tensor": tensor_at}

    offsets = peer_offsets(sizes, kinds)
    barrier = pltpu.get_barrier_semaphore()
    for offset in offsets:
        pl.semaphore_signal(
            barrier, inc=1, device_id=device(offset), device_id_type=pl.DeviceIdType.MESH
        )
    pl.semaphore_wait(barrier, len(offsets))

    started, used = [], [0]

    def put(source, target, offset):
        number = used[0]
        used[0] += 1
        copy = pltpu.make_async_remote_copy(
            src_ref=source,
            dst_ref=target,
            send_sem=send_sem.at[number],
            recv_sem=recv_sem.at[number],
            device_id=device(offset),
            device_id_type=pl.DeviceIdType.MESH,
        )
        copy.start()
        started.append(copy)
        return number

    def arrived(number, target, offset):
        pltpu.make_async_remote_copy(
            src_ref=target,
            dst_ref=target,
            send_sem=send_sem.at[number],
            recv_sem=recv_sem.at[number],
            device_id=device(offset),
            device_id_type=pl.DeviceIdType.MESH,
        ).wait_recv()

    partner = (0, 1, 0, 0)
    pending, own_copies = [], []
    first = {}
    for at, kind in enumerate(kinds):
        source, target = ins[at], outs[at]
        index = functools.partial(slot_of, kind, n_ctx)
        mine = index(*coords((0, 0, 0, 0)))
        if kind == "swap":
            for offset in direct_offsets(sizes, kind):
                number = put(source, target.at[offset[3] - 1], offset)
                pending.append((number, target.at[offset[3] - 1], offset))
            continue
        if kind in ("ctx", "dp", "all"):
            for offset in direct_offsets(sizes, kind):
                number = put(source.at[index(*coords(offset))], target.at[mine], offset)
                pending.append((number, target.at[index(*coords(offset, -1))], offset))
            own = pltpu.make_async_copy(source.at[mine], target.at[mine], own_sem.at[at])
        else:
            stage = []
            if kind == "wg":
                for step in range(1, n_ctx):
                    offset = (0, 0, step, 0)
                    stage.append((put(source, target.at[mine], offset), offset))
            crossing = []
            for step in range(1, n_outer):
                offset = (step, 0, 0, 0)
                crossing.append((put(source, target.at[mine], offset), offset, (0, 0, 0, 0)))
            pending.append(
                (put(source, target.at[mine], partner), target.at[index(*coords(partner, -1))], partner)
            )
            own = pltpu.make_async_copy(source, target.at[mine], own_sem.at[at])
            first[at] = (stage, crossing)
        own.start()
        own_copies.append(own)
    for at in first:
        target = outs[at]
        index = functools.partial(slot_of, kinds[at], n_ctx)
        stage, crossing = first[at]
        for number, offset in stage:
            slot = index(*coords(offset, -1))
            arrived(number, target.at[slot], offset)
            for step in range(1, n_outer):
                across = (step, 0, 0, 0)
                crossing.append((put(target.at[slot], target.at[slot], across), across, offset))
            both = (0, 1, offset[2], 0)
            pending.append(
                (put(target.at[slot], target.at[slot], partner), target.at[index(*coords(both, -1))], partner)
            )
    for at in first:
        target = outs[at]
        index = functools.partial(slot_of, kinds[at], n_ctx)
        for number, across, offset in first[at][1]:
            origin = (across[0], 0, offset[2], 0)
            slot = index(*coords(origin, -1))
            arrived(number, target.at[slot], across)
            both = (across[0], 1, offset[2], 0)
            pending.append(
                (put(target.at[slot], target.at[slot], partner), target.at[index(*coords(both, -1))], partner)
            )
    for number, target, offset in pending:
        arrived(number, target, offset)
    for own in own_copies:
        own.wait()
    for copy in started:
        copy.wait_send()


def slot_of(kind, n_ctx, dp_at, ctx_at, tensor_at):
    if kind == "ctx":
        return ctx_at
    if kind in ("dp", "dpg"):
        return dp_at
    return dp_at * n_ctx + ctx_at


def direct_offsets(sizes, kind):
    n_outer, n_core, n_ctx, n_tensor = sizes
    if kind == "swap":
        return [(0, 0, 0, step) for step in range(1, n_tensor)]
    if kind == "ctx":
        return [(0, 0, step, 0) for step in range(1, n_ctx)]
    ctx_steps = range(n_ctx) if kind == "all" else range(1)
    return [
        (o, c, k, 0) for k in ctx_steps for o in range(n_outer) for c in range(n_core) if o + c + k
    ]


def peer_offsets(sizes, kinds):
    n_outer, n_core, n_ctx, n_tensor = sizes
    found = set()
    for kind in kinds:
        if kind in ("wg", "dpg"):
            found.update((o, 0, 0, 0) for o in range(1, n_outer))
            found.add((0, 1, 0, 0))
            if kind == "wg":
                found.update((0, 0, k, 0) for k in range(1, n_ctx))
        else:
            found.update(direct_offsets(sizes, kind))
    return sorted(found)


def exchange(sizes, number, ops):
    n_outer, n_core, n_ctx, n_tensor = sizes
    n_dp = n_outer * n_core
    kinds = tuple(kind for kind, _ in ops)
    shapes, copies, moved = [], 0, 0
    for kind, array in ops:
        if kind == "swap":
            lead, sends = (n_tensor - 1,), n_tensor - 1
        elif kind == "dpg":
            lead, sends = (n_dp,), n_dp - 1
        elif kind == "wg":
            lead, sends = (n_dp * n_ctx,), n_dp * n_ctx - 1
        else:
            lead, sends = (), array.shape[0] - 1
        shapes.append(jax.ShapeDtypeStruct(lead + array.shape, array.dtype))
        copies += sends
        moved += math.prod(lead + array.shape) * array.dtype.itemsize
    vmem = pl.BlockSpec(memory_space=pltpu.VMEM)
    return pl.pallas_call(
        functools.partial(comm_kernel, sizes, kinds, copies),
        out_shape=tuple(shapes),
        in_specs=[vmem] * len(ops),
        out_specs=tuple(
            pl.BlockSpec(memory_space=pl.ANY) if kind == "wg" else vmem for kind in kinds
        ),
        scratch_shapes=[
            pltpu.SemaphoreType.DMA((copies,)),
            pltpu.SemaphoreType.DMA((copies,)),
            pltpu.SemaphoreType.DMA((len(ops),)),
        ],
        compiler_params=pltpu.CompilerParams(
            collective_id=number, has_side_effects=True, vmem_limit_bytes=60 * 2**20
        ),
        cost_estimate=pl.CostEstimate(
            flops=0, bytes_accessed=moved * 10, transcendentals=0
        ),
        name=f"exchange_{number}",
    )(*(array for _, array in ops))


def pack(parts, lead, unit):
    flat = jnp.concatenate([part.reshape(lead, -1) for part in parts], axis=1)
    wide = -(-flat.shape[1] // unit) * unit
    return jnp.pad(flat, ((0, 0), (0, wide - flat.shape[1]))).reshape(lead, wide // 128, 128)


def unpack(packed, shapes):
    flat = packed.reshape(packed.shape[0], -1)
    out, at = [], 0
    for shape in shapes:
        size = math.prod(shape)
        out.append(flat[:, at : at + size].reshape((packed.shape[0],) + shape))
        at += size
    return out


def on_device(
    sizes,
    tokens,
    seq_lengths,
    qkv_weight,
    out_weight,
    up_weight,
    down_weight,
    head_bias,
    hidden_bias,
    norm_gains,
    out_biases,
    cotangent,
):
    n_outer, n_core, n_ctx, n_tensor = sizes
    n_dp = n_outer * n_core
    shards = n_dp * n_ctx
    seq_count, local_len, width = tokens.shape
    row_count = seq_count * local_len
    total_len = n_ctx * local_len
    local_width = qkv_weight.shape[2]
    feature_rows = width // n_dp
    token_rows = tokens.reshape(row_count, width)

    def feature_slices(rows):
        return rows.reshape(row_count, n_dp, feature_rows).transpose(1, 0, 2)

    smalls = (head_bias, hidden_bias, norm_gains, out_biases)
    qkv_got, out_got, up_got, down_got, small_got, token_slices = exchange(
        sizes,
        1,
        [
            ("wg", qkv_weight.reshape(qkv_weight.shape[0], 3 * local_width)),
            ("wg", out_weight),
            ("wg", up_weight),
            ("wg", down_weight),
            ("wg", pack(smalls, 1, 2048)[0]),
            ("dp", feature_slices(token_rows)),
        ],
    )
    qkv_full = qkv_got.reshape(width, 3 * local_width)
    out_full = out_got.reshape(width, -1)
    up_full = up_got.reshape(width, -1)
    down_full = down_got.reshape(width, -1)
    head_full, hidden_full, gains_full, biases_full = (
        part.transpose(1, 0, 2).reshape(part.shape[1], -1)
        for part in unpack(small_got, [small.shape for small in smalls])
    )
    local_heads = head_full.shape[0]
    head_size = head_full.shape[1] // 2
    heads_here = local_heads // n_ctx
    group_width = heads_here * head_size
    bias_query = head_full[:, :head_size].reshape(local_width).astype(jnp.float32)
    bias_value = head_full[:, head_size:].reshape(local_width).astype(jnp.float32)
    bias_hidden = hidden_full.reshape(-1).astype(jnp.float32)
    gains_wide = gains_full.astype(jnp.float32)
    biases_wide = biases_full.astype(jnp.float32)

    def to_positions(chunks, parts):
        return (
            chunks.reshape(n_ctx, parts, seq_count, local_len, group_width)
            .transpose(1, 2, 0, 3, 4)
            .reshape(parts, seq_count, total_len, heads_here, head_size)
        )

    def by_position(parts):
        return (
            jnp.stack(parts)
            .reshape(len(parts), seq_count, n_ctx, local_len, group_width)
            .transpose(2, 0, 1, 3, 4)
            .reshape(n_ctx, len(parts), row_count, group_width)
        )

    def by_heads(rows, parts):
        return rows.reshape(row_count, parts, n_ctx, group_width).transpose(2, 1, 0, 3)

    def to_rows(chunks, parts):
        return (
            chunks.reshape(n_ctx, parts, row_count, group_width)
            .transpose(2, 1, 0, 3)
            .reshape(row_count, parts * local_width)
        )

    projected = jnp.dot(token_rows, qkv_full, preferred_element_type=jnp.float32)
    shift = jnp.concatenate([bias_query, jnp.zeros_like(bias_query), bias_value])
    projected = (projected + shift).astype(jnp.bfloat16)
    (qkv_chunks,) = exchange(sizes, 2, [("ctx", by_heads(projected, 3))])
    queries, key_rows, value_rows = to_positions(qkv_chunks, 3)
    valid = jnp.arange(total_len)[None, :] < seq_lengths[:, None]
    mixed, log_total = lax.map(attend_forward, (queries, key_rows, value_rows, valid))
    (mixed_chunks,) = exchange(sizes, 3, [("ctx", by_position([mixed]))])
    attn_flat = to_rows(mixed_chunks, 1)
    attn_part = contract_last(attn_flat, out_full)
    attn_other, attn_all = exchange(sizes, 4, [("swap", attn_part), ("dpg", attn_flat)])
    attn_proj = attn_part + jnp.sum(attn_other, axis=0)
    first_sum = token_rows.astype(jnp.float32) + attn_proj + biases_wide[0]
    normed_one, z_one, rstd_one = layer_norm(first_sum, gains_wide[0], biases_wide[1])
    normed_low = normed_one.astype(jnp.bfloat16)
    pre_act = jnp.dot(normed_low, up_full, preferred_element_type=jnp.float32) + bias_hidden
    activated, slope = gelu_parts(pre_act)
    hidden_low = activated.astype(jnp.bfloat16)
    mlp_part = contract_last(hidden_low, down_full)
    mlp_other, hidden_all, normed_slices = exchange(
        sizes,
        5,
        [("swap", mlp_part), ("dpg", hidden_low), ("dp", feature_slices(normed_low))],
    )
    mlp_out = mlp_part + jnp.sum(mlp_other, axis=0)
    second_sum = normed_one + mlp_out + biases_wide[2]
    result, z_two, rstd_two = layer_norm(second_sum, gains_wide[1], biases_wide[3])
    output = result.astype(jnp.bfloat16).reshape(seq_count, local_len, width)
    grad_out = cotangent.reshape(row_count, width).astype(jnp.float32)
    grad_two, gain_two_grad, shift_two_grad = norm_back(grad_out, z_two, rstd_two, gains_wide[1])
    grad_two_low = grad_two.astype(jnp.bfloat16)
    grad_hidden = jnp.dot(grad_two_low, down_full, preferred_element_type=jnp.float32)
    grad_pre = grad_hidden * slope
    grad_pre_low = grad_pre.astype(jnp.bfloat16)
    hidden_part = jnp.sum(grad_pre, axis=0).reshape(hidden_full.shape)
    normed_part = contract_last(grad_pre_low, up_full)
    normed_other, grad_pre_all, grad_two_slices = exchange(
        sizes,
        6,
        [("swap", normed_part), ("dpg", grad_pre_low), ("dp", feature_slices(grad_two_low))],
    )

    def over_rows(slices, wide):
        return contract_first(
            slices.reshape(n_dp * row_count, feature_rows), wide.reshape(n_dp * row_count, -1)
        )

    down_grad = lax.psum_scatter(
        over_rows(grad_two_slices, hidden_all), "ctx", scatter_dimension=0, tiled=True
    )
    up_grad = lax.psum_scatter(
        over_rows(normed_slices, grad_pre_all), "ctx", scatter_dimension=0, tiled=True
    )
    grad_normed = normed_part + jnp.sum(normed_other, axis=0) + grad_two
    grad_one, gain_one_grad, shift_one_grad = norm_back(grad_normed, z_one, rstd_one, gains_wide[0])
    grad_one_low = grad_one.astype(jnp.bfloat16)
    grad_attn = jnp.dot(grad_one_low, out_full, preferred_element_type=jnp.float32).astype(
        jnp.bfloat16
    )
    grad_chunks, grad_one_slices = exchange(
        sizes, 7, [("ctx", by_heads(grad_attn, 1)), ("dp", feature_slices(grad_one_low))]
    )
    grad_mixed = to_positions(grad_chunks, 1)[0]
    out_grad = over_rows(grad_one_slices, attn_all)
    grad_queries, grad_keys, grad_values = lax.map(
        attend_backward, (queries, key_rows, value_rows, valid, mixed, log_total, grad_mixed)
    )
    (proj_chunks,) = exchange(
        sizes,
        8,
        [
            (
                "ctx",
                by_position(
                    [part.astype(jnp.bfloat16) for part in (grad_queries, grad_keys, grad_values)]
                ),
            )
        ],
    )
    grad_proj = to_rows(proj_chunks, 3)
    input_part = contract_last(grad_proj, qkv_full)
    head_rows = jnp.concatenate(
        [jnp.sum(grad_queries, axis=(0, 1)), jnp.sum(grad_values, axis=(0, 1))], axis=1
    )
    head_part = lax.dynamic_update_slice(
        jnp.zeros((local_heads, 2 * head_size), jnp.float32),
        head_rows,
        (lax.axis_index("ctx") * heads_here, 0),
    )
    gains_part = jnp.stack([gain_one_grad, gain_two_grad])
    biases_part = jnp.stack(
        [jnp.sum(grad_one, axis=0), shift_one_grad, jnp.sum(grad_two, axis=0), shift_two_grad]
    )
    small_parts = [
        part.reshape(part.shape[0], shards, -1).transpose(1, 0, 2)
        for part in (head_part, hidden_part, gains_part, biases_part)
    ]
    input_other, proj_all, small_sums, out_blocks = exchange(
        sizes,
        9,
        [
            ("swap", input_part),
            ("dpg", grad_proj),
            ("all", pack(small_parts, shards, 1024)),
            ("ctx", out_grad.reshape(n_ctx, feature_rows // n_ctx, -1)),
        ],
    )
    input_grad = (input_part + jnp.sum(input_other, axis=0) + grad_one).reshape(
        seq_count, local_len, width
    )
    qkv_part = over_rows(token_slices, proj_all)
    (qkv_blocks,) = exchange(
        sizes, 10, [("ctx", qkv_part.reshape(n_ctx, feature_rows // n_ctx, -1))]
    )
    qkv_grad = jnp.sum(qkv_blocks, axis=0).reshape(-1, 3, local_width)
    small_grads = unpack(
        jnp.sum(small_sums, axis=0)[None], [part.shape[1:] for part in small_parts]
    )
    return (
        output,
        input_grad,
        qkv_grad,
        jnp.sum(out_blocks, axis=0),
        up_grad,
        down_grad,
        *(part[0] for part in small_grads),
    )


def solution(mesh):
    in_specs = (
        P("dp", "ctx", None),
        P("dp"),
        P(("dp", "ctx"), None, "tensor"),
        P(("dp", "ctx"), "tensor"),
        P(("dp", "ctx"), "tensor"),
        P(("dp", "ctx"), "tensor"),
        P("tensor", ("dp", "ctx")),
        P("tensor", ("dp", "ctx")),
        P(None, ("dp", "ctx")),
        P(None, ("dp", "ctx")),
        P("dp", "ctx", None),
    )
    out_specs = (
        P("dp", "ctx", None),
        P("dp", "ctx", None),
        P(("dp", "ctx"), None, "tensor"),
        P(("dp", "ctx"), "tensor"),
        P(("dp", "ctx"), "tensor"),
        P(("dp", "ctx"), "tensor"),
        P("tensor", ("dp", "ctx")),
        P("tensor", ("dp", "ctx")),
        P(None, ("dp", "ctx")),
        P(None, ("dp", "ctx")),
    )
    n_core = 2 if mesh.shape["dp"] % 2 == 0 else 1
    sizes = (mesh.shape["dp"] // n_core, n_core, mesh.shape["ctx"], mesh.shape["tensor"])
    return jax.shard_map(
        functools.partial(on_device, sizes), mesh=mesh, in_specs=in_specs, out_specs=out_specs, check_vma=False
    )
```

```python
import functools
import math

import jax
import jax.numpy as jnp
from jax import lax
from jax.experimental import pallas as pl
from jax.experimental.pallas import tpu as pltpu
from jax.sharding import PartitionSpec as P

EPSILON = 1e-05
SCALE = 0.125
NEG_BIG = -1000000000.0
INV_ROOT_TWO = 1.0 / math.sqrt(2.0)
INV_ROOT_TWO_PI = 1.0 / math.sqrt(2.0 * math.pi)


def contract_last(left, right):
    return lax.dot_general(
        left, right, (((1,), (1,)), ((), ())), preferred_element_type=jnp.float32
    )


def contract_first(left, right):
    return lax.dot_general(
        left, right, (((0,), (0,)), ((), ())), preferred_element_type=jnp.float32
    )


def layer_norm(hidden_in, gain, shift):
    centred = hidden_in - jnp.mean(hidden_in, axis=-1, keepdims=True)
    variance = jnp.mean(centred * centred, axis=-1, keepdims=True)
    inv_std = lax.rsqrt(variance + EPSILON)
    normed = centred * inv_std
    return (normed * gain + shift, normed, inv_std)


def norm_back(grad_out, normed, inv_std, gain):
    grad_normed = grad_out * gain
    first_mean = jnp.mean(grad_normed, axis=-1, keepdims=True)
    second_mean = jnp.mean(grad_normed * normed, axis=-1, keepdims=True)
    grad_in = inv_std * (grad_normed - first_mean - normed * second_mean)
    return (grad_in, jnp.sum(grad_out * normed, axis=0), jnp.sum(grad_out, axis=0))


def gelu_parts(pre_act):
    cdf_val = 0.5 * (1.0 + jax.scipy.special.erf(pre_act * INV_ROOT_TWO))
    return (
        pre_act * cdf_val,
        cdf_val + pre_act * jnp.exp(-0.5 * pre_act * pre_act) * INV_ROOT_TWO_PI,
    )


def block_scores(queries, key_rows, valid):
    scores = (
        jnp.einsum("qhd,khd->hqk", queries, key_rows, preferred_element_type=jnp.float32) * SCALE
    )
    return jnp.where(valid[None, None, :], scores, NEG_BIG)


def attend_forward(inputs):
    queries, key_rows, value_rows, valid = inputs
    scores = block_scores(queries, key_rows, valid)
    peak = jnp.max(scores, axis=-1, keepdims=True)
    log_total = peak + jnp.log(jnp.sum(jnp.exp(scores - peak), axis=-1, keepdims=True))
    probs = jnp.exp(scores - log_total).astype(jnp.bfloat16)
    mixed = jnp.einsum(
        "hqk,khd->qhd", probs, value_rows, preferred_element_type=jnp.float32
    ).astype(jnp.bfloat16)
    return (mixed, log_total)


def attend_backward(inputs):
    queries, key_rows, value_rows, valid, mixed, log_total, grad_mixed = inputs
    scores = block_scores(queries, key_rows, valid)
    probs = jnp.exp(scores - log_total)
    grad_values = jnp.einsum(
        "hqk,qhd->khd", probs.astype(jnp.bfloat16), grad_mixed, preferred_element_type=jnp.float32
    )
    grad_probs = jnp.einsum(
        "qhd,khd->hqk", grad_mixed, value_rows, preferred_element_type=jnp.float32
    )
    inner = jnp.einsum("qhd,qhd->hq", grad_mixed.astype(jnp.float32), mixed.astype(jnp.float32))
    grad_scores = (probs * (grad_probs - inner[:, :, None])).astype(jnp.bfloat16)
    grad_queries = (
        jnp.einsum("hqk,khd->qhd", grad_scores, key_rows, preferred_element_type=jnp.float32)
        * SCALE
    )
    grad_keys = (
        jnp.einsum("hqk,qhd->khd", grad_scores, queries, preferred_element_type=jnp.float32) * SCALE
    )
    return (grad_queries, grad_keys, grad_values)


def comm_kernel(sizes, kinds, copies, *refs):
    n_outer, n_core, n_ctx, n_tensor = sizes
    count = len(kinds)
    ins, outs = refs[:count], refs[count : 2 * count]
    send_sem, recv_sem, own_sem = refs[2 * count :]
    dp, ctx, tensor = (lax.axis_index(name) for name in ("dp", "ctx", "tensor"))
    outer, core = dp // n_core, dp % n_core

    def coords(offset, sign=1):
        def move(at, step, size):
            return at if step == 0 else (at + (step if sign > 0 else size - step)) % size

        outer_at = move(outer, offset[0], n_outer)
        core_at = move(core, offset[1], n_core)
        return outer_at * n_core + core_at, move(ctx, offset[2], n_ctx), move(tensor, offset[3], n_tensor)

    def device(offset):
        dp_at, ctx_at, tensor_at = coords(offset)
        return {"dp": dp_at, "ctx": ctx_at, "tensor": tensor_at}

    offsets = peer_offsets(sizes, kinds)
    barrier = pltpu.get_barrier_semaphore()
    for offset in offsets:
        pl.semaphore_signal(
            barrier, inc=1, device_id=device(offset), device_id_type=pl.DeviceIdType.MESH
        )
    pl.semaphore_wait(barrier, len(offsets))

    started, used = [], [0]

    def put(source, target, offset):
        number = used[0]
        used[0] += 1
        copy = pltpu.make_async_remote_copy(
            src_ref=source,
            dst_ref=target,
            send_sem=send_sem.at[number],
            recv_sem=recv_sem.at[number],
            device_id=device(offset),
            device_id_type=pl.DeviceIdType.MESH,
        )
        copy.start()
        started.append(copy)
        return number

    def arrived(number, target, offset):
        pltpu.make_async_remote_copy(
            src_ref=target,
            dst_ref=target,
            send_sem=send_sem.at[number],
            recv_sem=recv_sem.at[number],
            device_id=device(offset),
            device_id_type=pl.DeviceIdType.MESH,
        ).wait_recv()

    partner = (0, 1, 0, 0)
    pending, own_copies = [], []
    first = {}
    for at, kind in enumerate(kinds):
        source, target = ins[at], outs[at]
        index = functools.partial(slot_of, kind, n_ctx)
        mine = index(*coords((0, 0, 0, 0)))
        if kind == "swap":
            for offset in direct_offsets(sizes, kind):
                number = put(source, target.at[offset[3] - 1], offset)
                pending.append((number, target.at[offset[3] - 1], offset))
            continue
        if kind in ("ctx", "cg", "dp", "all"):
            for offset in direct_offsets(sizes, kind):
                block = source if kind == "cg" else source.at[index(*coords(offset))]
                number = put(block, target.at[mine], offset)
                pending.append((number, target.at[index(*coords(offset, -1))], offset))
            block = source if kind == "cg" else source.at[mine]
            own = pltpu.make_async_copy(block, target.at[mine], own_sem.at[at])
        else:
            stage = []
            if kind == "wg":
                for step in range(1, n_ctx):
                    offset = (0, 0, step, 0)
                    stage.append((put(source, target.at[mine], offset), offset))
            crossing = []
            for step in range(1, n_outer):
                offset = (step, 0, 0, 0)
                crossing.append((put(source, target.at[mine], offset), offset, (0, 0, 0, 0)))
            pending.append(
                (put(source, target.at[mine], partner), target.at[index(*coords(partner, -1))], partner)
            )
            own = pltpu.make_async_copy(source, target.at[mine], own_sem.at[at])
            first[at] = (stage, crossing)
        own.start()
        own_copies.append(own)
    for at in first:
        target = outs[at]
        index = functools.partial(slot_of, kinds[at], n_ctx)
        stage, crossing = first[at]
        for number, offset in stage:
            slot = index(*coords(offset, -1))
            arrived(number, target.at[slot], offset)
            for step in range(1, n_outer):
                across = (step, 0, 0, 0)
                crossing.append((put(target.at[slot], target.at[slot], across), across, offset))
            both = (0, 1, offset[2], 0)
            pending.append(
                (put(target.at[slot], target.at[slot], partner), target.at[index(*coords(both, -1))], partner)
            )
    for at in first:
        target = outs[at]
        index = functools.partial(slot_of, kinds[at], n_ctx)
        for number, across, offset in first[at][1]:
            origin = (across[0], 0, offset[2], 0)
            slot = index(*coords(origin, -1))
            arrived(number, target.at[slot], across)
            both = (across[0], 1, offset[2], 0)
            pending.append(
                (put(target.at[slot], target.at[slot], partner), target.at[index(*coords(both, -1))], partner)
            )
    for number, target, offset in pending:
        arrived(number, target, offset)
    for own in own_copies:
        own.wait()
    for copy in started:
        copy.wait_send()


def slot_of(kind, n_ctx, dp_at, ctx_at, tensor_at):
    if kind in ("ctx", "cg"):
        return ctx_at
    if kind in ("dp", "dpg"):
        return dp_at
    return dp_at * n_ctx + ctx_at


def direct_offsets(sizes, kind):
    n_outer, n_core, n_ctx, n_tensor = sizes
    if kind == "swap":
        return [(0, 0, 0, step) for step in range(1, n_tensor)]
    if kind in ("ctx", "cg"):
        return [(0, 0, step, 0) for step in range(1, n_ctx)]
    ctx_steps = range(n_ctx) if kind == "all" else range(1)
    return [
        (o, c, k, 0) for k in ctx_steps for o in range(n_outer) for c in range(n_core) if o + c + k
    ]


def peer_offsets(sizes, kinds):
    n_outer, n_core, n_ctx, n_tensor = sizes
    found = set()
    for kind in kinds:
        if kind in ("wg", "dpg"):
            found.update((o, 0, 0, 0) for o in range(1, n_outer))
            found.add((0, 1, 0, 0))
            if kind == "wg":
                found.update((0, 0, k, 0) for k in range(1, n_ctx))
        else:
            found.update(direct_offsets(sizes, kind))
    return sorted(found)


def exchange(sizes, number, ops):
    n_outer, n_core, n_ctx, n_tensor = sizes
    n_dp = n_outer * n_core
    kinds = tuple(kind for kind, _ in ops)
    shapes, copies, moved = [], 0, 0
    for kind, array in ops:
        if kind == "swap":
            lead, sends = (n_tensor - 1,), n_tensor - 1
        elif kind == "dpg":
            lead, sends = (n_dp,), n_dp - 1
        elif kind == "cg":
            lead, sends = (n_ctx,), n_ctx - 1
        elif kind == "wg":
            lead, sends = (n_dp * n_ctx,), n_dp * n_ctx - 1
        else:
            lead, sends = (), array.shape[0] - 1
        shapes.append(jax.ShapeDtypeStruct(lead + array.shape, array.dtype))
        copies += sends
        moved += math.prod(lead + array.shape) * array.dtype.itemsize
    vmem = pl.BlockSpec(memory_space=pltpu.VMEM)
    return pl.pallas_call(
        functools.partial(comm_kernel, sizes, kinds, copies),
        out_shape=tuple(shapes),
        in_specs=[vmem] * len(ops),
        out_specs=tuple(
            pl.BlockSpec(memory_space=pl.ANY) if kind == "wg" else vmem for kind in kinds
        ),
        scratch_shapes=[
            pltpu.SemaphoreType.DMA((copies,)),
            pltpu.SemaphoreType.DMA((copies,)),
            pltpu.SemaphoreType.DMA((len(ops),)),
        ],
        compiler_params=pltpu.CompilerParams(
            collective_id=number, has_side_effects=True, vmem_limit_bytes=60 * 2**20
        ),
        cost_estimate=pl.CostEstimate(
            flops=0, bytes_accessed=moved * 10, transcendentals=0
        ),
        name=f"exchange_{number}",
    )(*(array for _, array in ops))


def pack(parts, lead, unit):
    flat = jnp.concatenate([part.reshape(lead, -1) for part in parts], axis=1)
    wide = -(-flat.shape[1] // unit) * unit
    return jnp.pad(flat, ((0, 0), (0, wide - flat.shape[1]))).reshape(lead, wide // 128, 128)


def unpack(packed, shapes):
    flat = packed.reshape(packed.shape[0], -1)
    out, at = [], 0
    for shape in shapes:
        size = math.prod(shape)
        out.append(flat[:, at : at + size].reshape((packed.shape[0],) + shape))
        at += size
    return out


def on_device(
    sizes,
    tokens,
    seq_lengths,
    qkv_weight,
    out_weight,
    up_weight,
    down_weight,
    head_bias,
    hidden_bias,
    norm_gains,
    out_biases,
    cotangent,
):
    n_outer, n_core, n_ctx, n_tensor = sizes
    n_dp = n_outer * n_core
    shards = n_dp * n_ctx
    seq_count, local_len, width = tokens.shape
    row_count = seq_count * local_len
    total_len = n_ctx * local_len
    local_width = qkv_weight.shape[2]
    feature_rows = width // n_dp
    token_rows = tokens.reshape(row_count, width)

    def feature_slices(rows):
        return rows.reshape(row_count, n_dp, feature_rows).transpose(1, 0, 2)

    smalls = (head_bias, hidden_bias, norm_gains, out_biases)
    qkv_got, out_got, small_got, token_slices = exchange(
        sizes,
        1,
        [
            ("wg", qkv_weight.reshape(qkv_weight.shape[0], 3 * local_width)),
            ("wg", out_weight),
            ("wg", pack(smalls, 1, 2048)[0]),
            ("dp", feature_slices(token_rows)),
        ],
    )
    qkv_full = qkv_got.reshape(width, 3 * local_width)
    out_full = out_got.reshape(width, -1)
    up_full = lax.all_gather(up_weight, ("dp", "ctx"), axis=0, tiled=True)
    down_full = lax.all_gather(down_weight, ("dp", "ctx"), axis=0, tiled=True)
    head_full, hidden_full, gains_full, biases_full = (
        part.transpose(1, 0, 2).reshape(part.shape[1], -1)
        for part in unpack(small_got, [small.shape for small in smalls])
    )
    local_heads = head_full.shape[0]
    head_size = head_full.shape[1] // 2
    heads_here = local_heads // n_ctx
    group_width = heads_here * head_size
    bias_query = head_full[:, :head_size].reshape(local_width).astype(jnp.float32)
    bias_value = head_full[:, head_size:].reshape(local_width).astype(jnp.float32)
    bias_hidden = hidden_full.reshape(-1).astype(jnp.float32)
    gains_wide = gains_full.astype(jnp.float32)
    biases_wide = biases_full.astype(jnp.float32)

    def to_positions(chunks, parts):
        return (
            chunks.reshape(n_ctx, parts, seq_count, local_len, group_width)
            .transpose(1, 2, 0, 3, 4)
            .reshape(parts, seq_count, total_len, heads_here, head_size)
        )

    def by_position(parts):
        return (
            jnp.stack(parts)
            .reshape(len(parts), seq_count, n_ctx, local_len, group_width)
            .transpose(2, 0, 1, 3, 4)
            .reshape(n_ctx, len(parts), row_count, group_width)
        )

    def by_heads(rows, parts):
        return rows.reshape(row_count, parts, n_ctx, group_width).transpose(2, 1, 0, 3)

    def to_rows(chunks, parts):
        return (
            chunks.reshape(n_ctx, parts, row_count, group_width)
            .transpose(2, 1, 0, 3)
            .reshape(row_count, parts * local_width)
        )

    projected = jnp.dot(token_rows, qkv_full, preferred_element_type=jnp.float32)
    shift = jnp.concatenate([bias_query, jnp.zeros_like(bias_query), bias_value])
    projected = (projected + shift).astype(jnp.bfloat16)
    (qkv_chunks,) = exchange(sizes, 2, [("ctx", by_heads(projected, 3))])
    queries, key_rows, value_rows = to_positions(qkv_chunks, 3)
    valid = jnp.arange(total_len)[None, :] < seq_lengths[:, None]
    mixed, log_total = lax.map(attend_forward, (queries, key_rows, value_rows, valid))
    (mixed_chunks,) = exchange(sizes, 3, [("ctx", by_position([mixed]))])
    attn_flat = to_rows(mixed_chunks, 1)
    attn_part = contract_last(attn_flat, out_full)
    attn_other, attn_all = exchange(sizes, 4, [("swap", attn_part), ("dpg", attn_flat)])
    attn_proj = attn_part + jnp.sum(attn_other, axis=0)
    first_sum = token_rows.astype(jnp.float32) + attn_proj + biases_wide[0]
    normed_one, z_one, rstd_one = layer_norm(first_sum, gains_wide[0], biases_wide[1])
    normed_low = normed_one.astype(jnp.bfloat16)
    pre_act = jnp.dot(normed_low, up_full, preferred_element_type=jnp.float32) + bias_hidden
    activated, slope = gelu_parts(pre_act)
    hidden_low = activated.astype(jnp.bfloat16)
    mlp_part = contract_last(hidden_low, down_full)
    half = n_dp // 2
    mlp_other, hidden_all, token_low = exchange(
        sizes,
        5,
        [("swap", mlp_part), ("dpg", hidden_low), ("cg", token_slices[:half])],
    )
    mlp_out = mlp_part + jnp.sum(mlp_other, axis=0)
    second_sum = normed_one + mlp_out + biases_wide[2]
    result, z_two, rstd_two = layer_norm(second_sum, gains_wide[1], biases_wide[3])
    output = result.astype(jnp.bfloat16).reshape(seq_count, local_len, width)
    grad_out = cotangent.reshape(row_count, width).astype(jnp.float32)
    grad_two, gain_two_grad, shift_two_grad = norm_back(grad_out, z_two, rstd_two, gains_wide[1])
    grad_two_low = grad_two.astype(jnp.bfloat16)
    grad_hidden = jnp.dot(grad_two_low, down_full, preferred_element_type=jnp.float32)
    grad_pre = grad_hidden * slope
    grad_pre_low = grad_pre.astype(jnp.bfloat16)
    hidden_part = jnp.sum(grad_pre, axis=0).reshape(hidden_full.shape)
    normed_part = contract_last(grad_pre_low, up_full)
    normed_other, grad_pre_all, grad_two_slices, token_high = exchange(
        sizes,
        6,
        [
            ("swap", normed_part),
            ("dpg", grad_pre_low),
            ("dp", feature_slices(grad_two_low)),
            ("cg", token_slices[half:]),
        ],
    )

    def over_rows(slices, wide):
        return contract_first(
            slices.reshape(n_dp * row_count, feature_rows), wide.reshape(n_dp * row_count, -1)
        )

    down_grad = lax.psum_scatter(
        over_rows(grad_two_slices, hidden_all), "ctx", scatter_dimension=0, tiled=True
    )
    grad_normed = normed_part + jnp.sum(normed_other, axis=0) + grad_two
    grad_one, gain_one_grad, shift_one_grad = norm_back(grad_normed, z_one, rstd_one, gains_wide[0])
    grad_one_low = grad_one.astype(jnp.bfloat16)
    grad_attn = jnp.dot(grad_one_low, out_full, preferred_element_type=jnp.float32).astype(
        jnp.bfloat16
    )
    grad_chunks, grad_one_slices, normed_slices = exchange(
        sizes,
        7,
        [
            ("ctx", by_heads(grad_attn, 1)),
            ("dp", feature_slices(grad_one_low)),
            ("dp", feature_slices(normed_low)),
        ],
    )
    up_grad = lax.psum_scatter(
        over_rows(normed_slices, grad_pre_all), "ctx", scatter_dimension=0, tiled=True
    )
    grad_mixed = to_positions(grad_chunks, 1)[0]
    out_grad = over_rows(grad_one_slices, attn_all)
    grad_queries, grad_keys, grad_values = lax.map(
        attend_backward, (queries, key_rows, value_rows, valid, mixed, log_total, grad_mixed)
    )
    proj_parts = by_position(
        [part.astype(jnp.bfloat16) for part in (grad_queries, grad_keys, grad_values)]
    )
    proj_wide = proj_parts.transpose(0, 2, 1, 3).reshape(n_ctx * row_count, 3 * group_width)
    proj_chunks, proj_all = exchange(sizes, 8, [("ctx", proj_parts), ("dpg", proj_wide)])
    token_all = (
        jnp.concatenate([token_low, token_high], axis=1)
        .transpose(1, 0, 2, 3)
        .reshape(n_dp * n_ctx * row_count, feature_rows)
    )
    qkv_part = contract_first(token_all, proj_all.reshape(n_dp * n_ctx * row_count, -1))
    grad_proj = to_rows(proj_chunks, 3)
    input_part = contract_last(grad_proj, qkv_full)
    head_rows = jnp.concatenate(
        [jnp.sum(grad_queries, axis=(0, 1)), jnp.sum(grad_values, axis=(0, 1))], axis=1
    )
    head_part = lax.dynamic_update_slice(
        jnp.zeros((local_heads, 2 * head_size), jnp.float32),
        head_rows,
        (lax.axis_index("ctx") * heads_here, 0),
    )
    gains_part = jnp.stack([gain_one_grad, gain_two_grad])
    biases_part = jnp.stack(
        [jnp.sum(grad_one, axis=0), shift_one_grad, jnp.sum(grad_two, axis=0), shift_two_grad]
    )
    small_parts = [
        part.reshape(part.shape[0], shards, -1).transpose(1, 0, 2)
        for part in (head_part, hidden_part, gains_part, biases_part)
    ]
    input_other, small_sums, out_blocks, qkv_blocks = exchange(
        sizes,
        9,
        [
            ("swap", input_part),
            ("all", pack(small_parts, shards, 1024)),
            ("ctx", out_grad.reshape(n_ctx, feature_rows // n_ctx, -1)),
            ("ctx", qkv_part.reshape(n_ctx, feature_rows // n_ctx, -1)),
        ],
    )
    input_grad = (input_part + jnp.sum(input_other, axis=0) + grad_one).reshape(
        seq_count, local_len, width
    )
    qkv_grad = (
        qkv_blocks.reshape(n_ctx, -1, 3, group_width)
        .transpose(1, 2, 0, 3)
        .reshape(-1, 3, local_width)
    )
    small_grads = unpack(
        jnp.sum(small_sums, axis=0)[None], [part.shape[1:] for part in small_parts]
    )
    return (
        output,
        input_grad,
        qkv_grad,
        jnp.sum(out_blocks, axis=0),
        up_grad,
        down_grad,
        *(part[0] for part in small_grads),
    )


def solution(mesh):
    in_specs = (
        P("dp", "ctx", None),
        P("dp"),
        P(("dp", "ctx"), None, "tensor"),
        P(("dp", "ctx"), "tensor"),
        P(("dp", "ctx"), "tensor"),
        P(("dp", "ctx"), "tensor"),
        P("tensor", ("dp", "ctx")),
        P("tensor", ("dp", "ctx")),
        P(None, ("dp", "ctx")),
        P(None, ("dp", "ctx")),
        P("dp", "ctx", None),
    )
    out_specs = (
        P("dp", "ctx", None),
        P("dp", "ctx", None),
        P(("dp", "ctx"), None, "tensor"),
        P(("dp", "ctx"), "tensor"),
        P(("dp", "ctx"), "tensor"),
        P(("dp", "ctx"), "tensor"),
        P("tensor", ("dp", "ctx")),
        P("tensor", ("dp", "ctx")),
        P(None, ("dp", "ctx")),
        P(None, ("dp", "ctx")),
    )
    n_core = 2 if mesh.shape["dp"] % 2 == 0 else 1
    sizes = (mesh.shape["dp"] // n_core, n_core, mesh.shape["ctx"], mesh.shape["tensor"])
    return jax.shard_map(
        functools.partial(on_device, sizes), mesh=mesh, in_specs=in_specs, out_specs=out_specs, check_vma=False
    )
```
